32 devices in a mesh: row: 4 (over y, x), col: 8 (over z, core).
Axes of the slice: x: 2, y: 2, z: 4, core: 2. Of those that a mesh axis runs over, the one named last changes fastest.
Arguments:
- weights: bfloat16 [3072, 3072], P('col', 'row'), may hold values from -0.109375 to 0.109375
- weight_flags: int32 [24, 24], P('col', 'row'), may hold values from 0 to 1, as said below
- hamiltonian: bfloat16 [3072, 4096], P('row', 'col'), may hold values from -6 to 6
- ham_flags: int32 [24, 32], P('row', 'col'), may hold values from 0 to 1, as said below
Outputs:
- coupling: bfloat16 [3072, 4096], P('row', 'col')
The draws below stay inside these ranges and needn't reach their ends.
Inputs may be any that keep to these rules, and one draw needn't show every extreme that they name: `weight_flags`: 1 marks a stored block of W, 0 an absent one; the share of stored blocks differs from block row to block row. `ham_flags`: 1 marks a stored block of the slab, 0 an absent one; the share of stored blocks differs from block row to block row.
All inputs are finite; a program needn't handle non-finite values.
Results may differ from the reference program's by a relative error of at most 0.001.
Values may be sent and summed in bfloat16 or wider, within the bound.
A program may use at most 64 MiB of HBM per device.

```python
import jax
import jax.numpy as jnp
from jax import lax

BLOCK = 128
RB = 6
SC = 4
STEPS = 4
MB = 24
SB = 32
N = 3072
S = 4096
N_ROW = 4
N_COL = 8


def draw_weight_flags(key, part):
    row_ids = jnp.arange(MB, dtype=jnp.int32)[:, None]
    threshold = 30 + 65 * (row_ids * 7 % MB) // MB
    rolled = jax.random.randint(key, (MB, MB), 0, 100)
    return (rolled < threshold).astype(jnp.int32)


def draw_ham_flags(key, part):
    row_ids = jnp.arange(MB, dtype=jnp.int32)[:, None]
    threshold = 35 + 60 * ((row_ids * 5 + 3) % MB) // MB
    rolled = jax.random.randint(jax.random.fold_in(key, 11), (MB, SB), 0, 100)
    return (rolled < threshold).astype(jnp.int32)


def steps_of(stream_key, dims, cuts, least, high):
    def one(position, parts):
        steps = jax.random.uniform(jax.random.fold_in(jax.random.fold_in(stream_key, 6), position), (parts,), jnp.float32, least / len(cuts), high / len(cuts))
        return jnp.repeat(jnp.exp(steps), dims[position] // parts).reshape((-1,) + (1,) * (len(dims) - position - 1))

    loudness = one(*cuts[0])
    for cut in cuts[1:]:
        loudness = loudness * one(*cut)
    return loudness


def normal_values(stream_key, shape, scale, bound, shards=(), kind=jnp.bfloat16):
    loudness = steps_of(stream_key, shape, shards, -0.22, 0.18) if shards else 1.0
    entries = jax.random.normal(stream_key, shape, jnp.float32) * scale * loudness
    return jnp.minimum(jnp.maximum(entries, -bound), bound).astype(kind)


def setup_inputs(seed: int = 0) -> dict:
    streams_of = jax.random.split(jax.random.key(seed), 5)
    return {
        "weights": normal_values(streams_of[0], (N, N), (STEPS * RB * BLOCK) ** -0.5, 0.109375, ((0, 8), (1, 4))),
        "weight_flags": draw_weight_flags(jax.random.fold_in(streams_of[4], 71), 0),
        "hamiltonian": normal_values(streams_of[2], (N, S), 1.0, 6.0, ((0, 4), (1, 8))),
        "ham_flags": draw_ham_flags(jax.random.fold_in(streams_of[4], 71), 0),
    }


def masked(dense_tile, flag_grid):
    row_blocks, col_blocks = flag_grid.shape
    block_edge = dense_tile.shape[0] // row_blocks
    shaped = dense_tile.reshape(row_blocks, block_edge, col_blocks, block_edge)
    retain = (flag_grid > 0)[:, None, :, None]
    return jnp.where(retain, shaped, jnp.zeros_like(shaped)).reshape(dense_tile.shape)


def reference(weights, weight_flags, hamiltonian, ham_flags):
    w_masked = masked(weights, weight_flags)
    h_masked = masked(hamiltonian, ham_flags)
    panel_rows = RB * BLOCK
    pair_count = N_COL // 2
    w_panels = w_masked.reshape(N_ROW, panel_rows, N_ROW, panel_rows)
    h_panels = h_masked.reshape(N_ROW, panel_rows, pair_count, 2 * SC * BLOCK)
    pair_ids = jnp.arange(pair_count, dtype=jnp.int32)

    def one_piece(piece_index):
        w_piece = lax.dynamic_index_in_dim(w_panels, piece_index, 2, keepdims=False)
        summed = jnp.zeros((pair_count, panel_rows, 2 * SC * BLOCK), jnp.float32)
        for step_index in range(STEPS):
            chosen = ((piece_index + pair_ids + step_index) % N_ROW).astype(jnp.int32)
            w_chosen = w_piece[chosen].astype(jnp.float32)
            h_chosen = h_panels[chosen, :, pair_ids, :].astype(jnp.float32)
            summed = summed + jnp.einsum("pkm,pkn->pmn", w_chosen, h_chosen, precision=lax.Precision.HIGHEST)
        return jnp.transpose(summed, (1, 0, 2)).reshape(panel_rows, pair_count * 2 * SC * BLOCK)

    pieces = lax.map(one_piece, jnp.arange(N_ROW, dtype=jnp.int32))
    return pieces.reshape(N, S).astype(jnp.bfloat16)
```

```python
import functools

import jax
import jax.numpy as jnp
from jax import lax
from jax.experimental import pallas as pl
from jax.experimental.pallas import tpu as pltpu
from jax.sharding import PartitionSpec as P

STEPS = 4


def from_behind(block, axis, distance):
    devices = range(lax.axis_size(axis))
    route = [((i - distance) % len(devices), i) for i in devices]
    return lax.ppermute(block, axis, route)


def from_partner(value, axis, bit):
    mask = 2**bit
    pairs = [(source, source ^ mask) for source in range(lax.axis_size(axis))]
    return lax.ppermute(value, axis, pairs)


def masked(dense_tile, flag_grid):
    row_blocks, col_blocks = flag_grid.shape
    block_edge = dense_tile.shape[0] // row_blocks
    shaped = dense_tile.reshape(row_blocks, block_edge, col_blocks, block_edge)
    retain = (flag_grid > 0)[:, None, :, None]
    return jnp.where(retain, shaped, jnp.zeros_like(shaped)).reshape(dense_tile.shape)


def aligned(operand, amount, bit_count, mover):
    for level in range(bit_count):
        moved = mover(operand, level)
        chosen = (amount >> level) % 2 == 1
        operand = jnp.where(chosen, moved, operand)
    return operand


def contract(left_part, right_part):
    return lax.dot_general(
        left_part, right_part, (((0,), (0,)), ((), ())), preferred_element_type=jnp.float32
    )


def shards(weights, weight_flags, hamiltonian, ham_flags):
    row_count = lax.axis_size("row")
    bit_count = (row_count - 1).bit_length()
    row_index = lax.axis_index("row")
    col_index = lax.axis_index("col")
    pair_index = col_index // 2
    parity = col_index % 2
    w_masked = masked(weights, weight_flags)
    h_masked = masked(hamiltonian, ham_flags)
    ham_tile = aligned(
        h_masked,
        pair_index,
        bit_count,
        lambda operand, level: from_behind(operand, "row", -(1 << level)),
    )
    w_half = aligned(
        w_masked,
        row_index,
        bit_count,
        lambda operand, level: from_behind(operand, "col", -(2 << level)),
    )
    half_rows = ham_tile.shape[0] // 2
    upper_rows = ham_tile[:half_rows]
    lower_rows = ham_tile[half_rows:]
    retained = jnp.where(parity == 0, upper_rows, lower_rows)
    handed = jnp.where(parity == 0, lower_rows, upper_rows)
    received = from_partner(handed, "col", 0)
    joined = jnp.where(
        parity == 0,
        jnp.concatenate((retained, received), 1),
        jnp.concatenate((received, retained), 1),
    )
    summed = contract(w_half, joined)
    for step_index in range(1, STEPS):
        w_half = from_behind(w_half, "col", -2)
        joined = from_behind(joined, "row", -1)
        summed = summed + contract(w_half, joined)
    half_width = summed.shape[1] // 2
    own_part = jnp.where(parity == 0, summed[:, :half_width], summed[:, half_width:])
    their_part = jnp.where(parity == 0, summed[:, half_width:], summed[:, :half_width])
    summed = own_part + from_partner(their_part, "col", 0)
    return summed.astype(jnp.bfloat16)


CHUNKS = 6
MESH = pl.DeviceIdType.MESH


def put(source, target, sent, landed, device):
    return pltpu.make_async_remote_copy(
        src_ref=source,
        dst_ref=target,
        send_sem=sent,
        recv_sem=landed,
        device_id=device,
        device_id_type=MESH,
    )


def gather_kernel(
    panels, w_flags, h_flags, w_ref, h_ref, out_ref, w_buf, h_buf, total,
    w_landed, up_sent, down_sent, core_sent, h_landed, h_sent,
):
    row = lax.axis_index("row")
    col = lax.axis_index("col")
    pair = col // 2
    core = col % 2
    partner = (row, pair * 2 + 1 - core)
    above = (row, col + 2)
    below = (row, col - 2)
    beside = row + 1 - 2 * (row % 2)
    across = (row + panels // 2) % panels
    opposite = (beside + panels // 2) % panels
    has_above = pair < panels - 1
    has_below = pair > 0

    barrier = pltpu.get_barrier_semaphore()

    def greet(device):
        pl.semaphore_signal(barrier, inc=1, device_id=device, device_id_type=MESH)

    greet(partner)
    greet((beside, col))
    greet((across, col))

    @pl.when(has_above)
    def _():
        greet(above)

    @pl.when(has_below)
    def _():
        greet(below)

    chunk_rows, width = w_buf.shape[3], w_buf.shape[4]
    edge = w_ref.shape[0] // w_flags.shape[0]
    for k in range(CHUNKS):
        for c in range(w_flags.shape[1]):
            lanes = slice(c * edge, (c + 1) * edge)
            for start in range(k * chunk_rows, (k + 1) * chunk_rows, min(edge, chunk_rows)):
                rows = slice(start, start + min(edge, chunk_rows))
                block = w_ref[rows, lanes]
                keep = w_flags[start // edge, c] > 0
                inner = slice(start - k * chunk_rows, start - k * chunk_rows + min(edge, chunk_rows))
                w_buf[pair, core, k, inner, lanes] = jnp.where(keep, block, jnp.zeros_like(block))
    half_rows = h_buf.shape[2]
    for r in range(h_flags.shape[0]):
        for c in range(h_flags.shape[1]):
            lanes = slice(c * edge, (c + 1) * edge)
            block = h_ref[r * edge:(r + 1) * edge, lanes]
            half, start = divmod(r * edge, half_rows)
            kept = jnp.where(h_flags[r, c] > 0, block, jnp.zeros_like(block))
            h_buf[row, half, start:start + edge, lanes] = kept

    pl.semaphore_wait(
        barrier, 3 + has_above.astype(jnp.int32) + has_below.astype(jnp.int32)
    )

    def go_up(panel, k):
        slot = w_buf.at[panel, core, k]
        return put(slot, slot, up_sent.at[panel, k], w_landed.at[panel, core, k], above)

    def go_down(panel, k):
        slot = w_buf.at[panel, core, k]
        return put(slot, slot, down_sent.at[panel, k], w_landed.at[panel, core, k], below)

    def go_over(panel, k):
        slot = w_buf.at[panel, core, k]
        return put(slot, slot, core_sent.at[panel, k], w_landed.at[panel, core, k], partner)

    def arrival(panel, half, k):
        slot = w_buf.at[panel, half, k]
        return put(slot, slot, core_sent.at[panel, k], w_landed.at[panel, half, k], partner)

    def h_put(panel, half, number, device):
        slot = h_buf.at[panel, half]
        return put(slot, slot, h_sent.at[number], h_landed.at[panel, half], device)

    def each(body):
        def step(k, carry):
            body(k)
            return carry

        lax.fori_loop(0, CHUNKS, step, 0)

    def first_sends(k):
        @pl.when(has_above)
        def _():
            go_up(pair, k).start()

        @pl.when(has_below)
        def _():
            go_down(pair, k).start()

    each(first_sends)
    h_copies = [
        h_put(row, 0, 0, (beside, col)),
        h_put(row, 1, 1, (across, col)),
        h_put(row, 1, 2, (beside, col)),
        h_put(row, 0, 3, (across, col)),
    ]
    for copy in h_copies:
        copy.start()
    each(lambda k: go_over(pair, k).start())

    def relay(distance, k):
        @pl.when(pair >= distance)
        def _():
            panel = pair - distance
            arrival(panel, core, k).wait_recv()

            @pl.when(has_above)
            def _():
                go_up(panel, k).start()

            go_over(panel, k).start()

        @pl.when(pair + distance < panels)
        def _():
            panel = pair + distance
            arrival(panel, core, k).wait_recv()

            @pl.when(has_below)
            def _():
                go_down(panel, k).start()

            go_over(panel, k).start()

    each(functools.partial(relay, 1))
    h_put(beside, 0, 0, (beside, col)).wait_recv()
    relay_across = h_put(beside, 0, 4, (across, col))
    relay_across.start()
    h_put(across, 1, 0, (beside, col)).wait_recv()
    relay_beside = h_put(across, 1, 5, (beside, col))
    relay_beside.start()
    for distance in range(2, panels - 1):
        each(functools.partial(relay, distance))
    h_put(beside, 1, 0, (beside, col)).wait_recv()
    h_put(across, 0, 0, (beside, col)).wait_recv()
    h_put(opposite, 0, 0, (beside, col)).wait_recv()
    h_put(opposite, 1, 0, (beside, col)).wait_recv()

    total[...] = jnp.zeros_like(total)
    span = CHUNKS * chunk_rows

    def near_panel(step, carry):
        panel = (pair + step) % panels
        gap = panel - pair

        @pl.when((gap < panels - 1) & (gap > 1 - panels))
        def _():
            each(lambda k: arrival(panel, 1 - core, k).wait_recv())
            left = w_buf[panel].reshape(2 * span, width)
            right = h_buf[panel].reshape(2 * span, h_buf.shape[3])
            total[...] += contract(left, right)

        return carry

    lax.fori_loop(0, panels, near_panel, 0)

    @pl.when((pair == 0) | (pair == panels - 1))
    def _():
        panel = panels - 1 - pair

        def far_chunk(k):
            arrival(panel, core, k).wait_recv()
            go_over(panel, k).start()
            rows = pl.ds(pl.multiple_of(k * chunk_rows, chunk_rows), chunk_rows)
            total[...] += contract(w_buf[panel, core, k], h_buf[panel, core, rows, :])
            arrival(panel, 1 - core, k).wait_recv()
            total[...] += contract(w_buf[panel, 1 - core, k], h_buf[panel, 1 - core, rows, :])

        each(far_chunk)

    out_ref[...] = total[...].astype(out_ref.dtype)

    for copy in h_copies + [relay_across, relay_beside]:
        copy.wait_send()

    def drain(panel, carry):
        def one(k):
            go_over(panel, k).wait_send()

            @pl.when(has_above & (panel <= pair))
            def _():
                go_up(panel, k).wait_send()

            @pl.when(has_below & (panel >= pair))
            def _():
                go_down(panel, k).wait_send()

        each(one)
        return carry

    lax.fori_loop(0, panels, drain, 0)


def gathered(weights, weight_flags, hamiltonian, ham_flags):
    panels = lax.axis_size("row")
    half_rows, width = weights.shape
    panel_rows, slice_cols = hamiltonian.shape
    dma = pltpu.SemaphoreType.DMA
    vmem = pl.BlockSpec(memory_space=pltpu.VMEM)
    smem = pl.BlockSpec(memory_space=pltpu.SMEM)
    return pl.pallas_call(
        functools.partial(gather_kernel, panels),
        out_shape=jax.ShapeDtypeStruct((width, slice_cols), jnp.bfloat16),
        in_specs=[smem, smem, vmem, vmem],
        out_specs=vmem,
        scratch_shapes=[
            pltpu.VMEM((panels, 2, CHUNKS, half_rows // CHUNKS, width), jnp.bfloat16),
            pltpu.VMEM((panels, 2, panel_rows // 2, slice_cols), jnp.bfloat16),
            pltpu.VMEM((width, slice_cols), jnp.float32),
            dma((panels, 2, CHUNKS)),
            dma((panels, CHUNKS)),
            dma((panels, CHUNKS)),
            dma((panels, CHUNKS)),
            dma((panels, 2)),
            dma((6,)),
        ],
        compiler_params=pltpu.CompilerParams(collective_id=0, has_side_effects=True),
    )(weight_flags, ham_flags, weights, hamiltonian)


def solution(mesh):
    placed = (P("col", "row"), P("col", "row"), P("row", "col"), P("row", "col"))
    every_panel = mesh.shape["row"] == STEPS and mesh.shape["col"] == 2 * STEPS
    return jax.shard_map(
        gathered if every_panel else shards,
        mesh=mesh, in_specs=placed, out_specs=P("row", "col"), check_vma=False,
    )
```

```python
import functools

import jax
import jax.numpy as jnp
from jax import lax
from jax.experimental import pallas as pl
from jax.experimental.pallas import tpu as pltpu
from jax.sharding import PartitionSpec as P

STEPS = 4


def from_behind(block, axis, distance):
    devices = range(lax.axis_size(axis))
    route = [((i - distance) % len(devices), i) for i in devices]
    return lax.ppermute(block, axis, route)


def from_partner(value, axis, bit):
    mask = 2**bit
    pairs = [(source, source ^ mask) for source in range(lax.axis_size(axis))]
    return lax.ppermute(value, axis, pairs)


def masked(dense_tile, flag_grid):
    row_blocks, col_blocks = flag_grid.shape
    block_edge = dense_tile.shape[0] // row_blocks
    shaped = dense_tile.reshape(row_blocks, block_edge, col_blocks, block_edge)
    retain = (flag_grid > 0)[:, None, :, None]
    return jnp.where(retain, shaped, jnp.zeros_like(shaped)).reshape(dense_tile.shape)


def aligned(operand, amount, bit_count, mover):
    for level in range(bit_count):
        moved = mover(operand, level)
        chosen = (amount >> level) % 2 == 1
        operand = jnp.where(chosen, moved, operand)
    return operand


def contract(left_part, right_part):
    return lax.dot_general(
        left_part, right_part, (((0,), (0,)), ((), ())), preferred_element_type=jnp.float32
    )


def shards(weights, weight_flags, hamiltonian, ham_flags):
    row_count = lax.axis_size("row")
    bit_count = (row_count - 1).bit_length()
    row_index = lax.axis_index("row")
    col_index = lax.axis_index("col")
    pair_index = col_index // 2
    parity = col_index % 2
    w_masked = masked(weights, weight_flags)
    h_masked = masked(hamiltonian, ham_flags)
    ham_tile = aligned(
        h_masked,
        pair_index,
        bit_count,
        lambda operand, level: from_behind(operand, "row", -(1 << level)),
    )
    w_half = aligned(
        w_masked,
        row_index,
        bit_count,
        lambda operand, level: from_behind(operand, "col", -(2 << level)),
    )
    half_rows = ham_tile.shape[0] // 2
    upper_rows = ham_tile[:half_rows]
    lower_rows = ham_tile[half_rows:]
    retained = jnp.where(parity == 0, upper_rows, lower_rows)
    handed = jnp.where(parity == 0, lower_rows, upper_rows)
    received = from_partner(handed, "col", 0)
    joined = jnp.where(
        parity == 0,
        jnp.concatenate((retained, received), 1),
        jnp.concatenate((received, retained), 1),
    )
    summed = contract(w_half, joined)
    for step_index in range(1, STEPS):
        w_half = from_behind(w_half, "col", -2)
        joined = from_behind(joined, "row", -1)
        summed = summed + contract(w_half, joined)
    half_width = summed.shape[1] // 2
    own_part = jnp.where(parity == 0, summed[:, :half_width], summed[:, half_width:])
    their_part = jnp.where(parity == 0, summed[:, half_width:], summed[:, :half_width])
    summed = own_part + from_partner(their_part, "col", 0)
    return summed.astype(jnp.bfloat16)


SHARES = (1, 1, 1)
CHUNKS = len(SHARES)
MESH = pl.DeviceIdType.MESH


def put(source, target, sent, landed, device):
    return pltpu.make_async_remote_copy(
        src_ref=source,
        dst_ref=target,
        send_sem=sent,
        recv_sem=landed,
        device_id=device,
        device_id_type=MESH,
    )


def gather_kernel(
    panels, w_flags_hbm, h_flags_hbm, w_hbm, h_hbm, out_ref, w_flags, h_flags, w_ref, h_ref, w_buf, h_buf, total,
    loaded, w_landed, up_sent, down_sent, core_sent, h_landed, h_sent,
):
    row = lax.axis_index("row")
    col = lax.axis_index("col")
    pair = col // 2
    core = col % 2
    partner = (row, pair * 2 + 1 - core)
    above = (row, col + 2)
    below = (row, col - 2)
    beside = row + 1 - 2 * (row % 2)
    across = (row + panels // 2) % panels
    opposite = (beside + panels // 2) % panels
    has_above = pair < panels - 1
    has_below = pair > 0

    loads = [
        pltpu.make_async_copy(source, target, loaded.at[n])
        for n, (source, target) in enumerate(
            ((w_flags_hbm, w_flags), (w_hbm, w_ref), (h_flags_hbm, h_flags), (h_hbm, h_ref))
        )
    ]
    for load in loads:
        load.start()

    barrier = pltpu.get_barrier_semaphore()

    def greet(device):
        pl.semaphore_signal(barrier, inc=1, device_id=device, device_id_type=MESH)

    greet(partner)
    greet((beside, col))
    greet((across, col))

    @pl.when(has_above)
    def _():
        greet(above)

    @pl.when(has_below)
    def _():
        greet(below)

    loads[0].wait()
    loads[1].wait()
    half_rows, width = w_ref.shape
    edge = half_rows // w_flags.shape[0]
    bounds = [half_rows * sum(SHARES[:k]) // sum(SHARES) for k in range(CHUNKS + 1)]
    for r in range(w_flags.shape[0]):
        for c in range(w_flags.shape[1]):
            rows, lanes = slice(r * edge, (r + 1) * edge), slice(c * edge, (c + 1) * edge)
            block = w_ref[rows, lanes]
            kept = jnp.where(w_flags[r, c] > 0, block, jnp.zeros_like(block))
            w_buf[pair, core, rows, lanes] = kept
    loads[2].wait()
    loads[3].wait()
    for r in range(h_flags.shape[1]):
        for c in range(h_flags.shape[0]):
            lanes = slice(c * edge, (c + 1) * edge)
            block = h_ref[r * edge:(r + 1) * edge, lanes]
            half, start = divmod(r * edge, half_rows)
            kept = jnp.where(h_flags[c, r] > 0, block, jnp.zeros_like(block))
            h_buf[row, half, start:start + edge, lanes] = kept

    pl.semaphore_wait(
        barrier, 3 + has_above.astype(jnp.int32) + has_below.astype(jnp.int32)
    )

    def piece(k):
        return slice(bounds[k], bounds[k + 1])

    def go_up(panel, k):
        slot = w_buf.at[panel, core, piece(k)]
        return put(slot, slot, up_sent.at[panel, k], w_landed.at[panel, core, k], above)

    def go_down(panel, k):
        slot = w_buf.at[panel, core, piece(k)]
        return put(slot, slot, down_sent.at[panel, k], w_landed.at[panel, core, k], below)

    def go_over(panel, k):
        slot = w_buf.at[panel, core, piece(k)]
        return put(slot, slot, core_sent.at[panel, k], w_landed.at[panel, core, k], partner)

    def arrival(panel, half, k):
        slot = w_buf.at[panel, half, piece(k)]
        return put(slot, slot, core_sent.at[panel, k], w_landed.at[panel, half, k], partner)

    def h_put(panel, half, number, device):
        slot = h_buf.at[panel, half]
        return put(slot, slot, h_sent.at[number], h_landed.at[panel, half], device)

    def each(body):
        for k in range(CHUNKS):
            body(k)

    def first_sends(k):
        @pl.when(has_above)
        def _():
            go_up(pair, k).start()

        @pl.when(has_below)
        def _():
            go_down(pair, k).start()

    each(first_sends)
    h_copies = [
        h_put(row, 0, 0, (beside, col)),
        h_put(row, 1, 1, (across, col)),
        h_put(row, 1, 2, (beside, col)),
        h_put(row, 0, 3, (across, col)),
    ]
    for copy in h_copies:
        copy.start()
    each(lambda k: go_over(pair, k).start())

    def relay(distance, k):
        @pl.when(pair >= distance)
        def _():
            panel = pair - distance
            arrival(panel, core, k).wait_recv()

            @pl.when(has_above)
            def _():
                go_up(panel, k).start()

            go_over(panel, k).start()

        @pl.when(pair + distance < panels)
        def _():
            panel = pair + distance
            arrival(panel, core, k).wait_recv()

            @pl.when(has_below)
            def _():
                go_down(panel, k).start()

            go_over(panel, k).start()

    each(functools.partial(relay, 1))
    h_put(beside, 0, 0, (beside, col)).wait_recv()
    relay_across = h_put(beside, 0, 4, (across, col))
    relay_across.start()
    h_put(across, 1, 0, (beside, col)).wait_recv()
    relay_beside = h_put(across, 1, 5, (beside, col))
    relay_beside.start()
    for distance in range(2, panels - 1):
        each(functools.partial(relay, distance))
    h_put(beside, 1, 0, (beside, col)).wait_recv()
    h_put(across, 0, 0, (beside, col)).wait_recv()
    h_put(opposite, 0, 0, (beside, col)).wait_recv()
    h_put(opposite, 1, 0, (beside, col)).wait_recv()

    total[...] = jnp.zeros_like(total)
    span = 2 * half_rows

    def near_panel(step, carry):
        panel = (pair + step) % panels
        gap = panel - pair

        @pl.when((gap < panels - 1) & (gap > 1 - panels))
        def _():
            each(lambda k: arrival(panel, 1 - core, k).wait_recv())
            left = w_buf[panel].reshape(span, width)
            right = h_buf[panel].reshape(span, h_buf.shape[3])
            total[...] += contract(left, right)

        return carry

    lax.fori_loop(0, panels, near_panel, 0)

    is_end = (pair == 0) | (pair == panels - 1)

    @pl.when(is_end)
    def _():
        panel = panels - 1 - pair

        def product(half, k):
            return contract(w_buf[panel, half, piece(k)], h_buf[panel, half, piece(k)])

        for k in range(CHUNKS - 1):
            arrival(panel, core, k).wait_recv()
            go_over(panel, k).start()
            total[...] += product(core, k)
            arrival(panel, 1 - core, k).wait_recv()
            total[...] += product(1 - core, k)

        last = CHUNKS - 1
        arrival(panel, core, last).wait_recv()
        go_over(panel, last).start()
        total[...] += product(core, last)
        arrival(panel, 1 - core, last).wait_recv()
        out_ref[...] = (total[...] + product(1 - core, last)).astype(out_ref.dtype)

    @pl.when(jnp.logical_not(is_end))
    def _():
        out_ref[...] = total[...].astype(out_ref.dtype)

    for copy in h_copies + [relay_across, relay_beside]:
        copy.wait_send()

    def drain(panel, carry):
        def one(k):
            go_over(panel, k).wait_send()

            @pl.when(has_above & (panel <= pair))
            def _():
                go_up(panel, k).wait_send()

            @pl.when(has_below & (panel >= pair))
            def _():
                go_down(panel, k).wait_send()

        each(one)
        return carry

    lax.fori_loop(0, panels, drain, 0)


def gathered(weights, weight_flags, hamiltonian, ham_flags):
    panels = lax.axis_size("row")
    half_rows, width = weights.shape
    panel_rows, slice_cols = hamiltonian.shape
    dma = pltpu.SemaphoreType.DMA
    vmem = pl.BlockSpec(memory_space=pltpu.VMEM)
    hbm = pl.BlockSpec(memory_space=pl.ANY)
    return pl.pallas_call(
        functools.partial(gather_kernel, panels),
        out_shape=pltpu.VMEM((width, slice_cols), jnp.bfloat16),
        in_specs=[hbm] * 4,
        out_specs=vmem,
        scratch_shapes=[
            pltpu.SMEM(weight_flags.shape, weight_flags.dtype),
            pltpu.SMEM(ham_flags.shape[::-1], ham_flags.dtype),
            pltpu.VMEM(weights.shape, weights.dtype),
            pltpu.VMEM(hamiltonian.shape, hamiltonian.dtype),
            pltpu.VMEM((panels, 2, half_rows, width), jnp.bfloat16),
            pltpu.VMEM((panels, 2, panel_rows // 2, slice_cols), jnp.bfloat16),
            pltpu.VMEM((width, slice_cols), jnp.float32),
            dma((4,)),
            dma((panels, 2, CHUNKS)),
            dma((panels, CHUNKS)),
            dma((panels, CHUNKS)),
            dma((panels, CHUNKS)),
            dma((panels, 2)),
            dma((6,)),
        ],
        compiler_params=pltpu.CompilerParams(collective_id=0, has_side_effects=True),
    )(weight_flags, ham_flags.T, weights, hamiltonian)


def solution(mesh):
    placed = (P("col", "row"), P("col", "row"), P("row", "col"), P("row", "col"))
    every_panel = mesh.shape["row"] == STEPS and mesh.shape["col"] == 2 * STEPS
    return jax.shard_map(
        gathered if every_panel else shards,
        mesh=mesh, in_specs=placed, out_specs=P("row", "col"), check_vma=False,
    )
```

```python
import functools

import jax
import jax.numpy as jnp
from jax import lax
from jax.experimental import pallas as pl
from jax.experimental.pallas import tpu as pltpu
from jax.sharding import PartitionSpec as P

STEPS = 4


def from_behind(block, axis, distance):
    devices = range(lax.axis_size(axis))
    route = [((i - distance) % len(devices), i) for i in devices]
    return lax.ppermute(block, axis, route)


def from_partner(value, axis, bit):
    mask = 2**bit
    pairs = [(source, source ^ mask) for source in range(lax.axis_size(axis))]
    return lax.ppermute(value, axis, pairs)


def masked(dense_tile, flag_grid):
    row_blocks, col_blocks = flag_grid.shape
    block_edge = dense_tile.shape[0] // row_blocks
    shaped = dense_tile.reshape(row_blocks, block_edge, col_blocks, block_edge)
    retain = (flag_grid > 0)[:, None, :, None]
    return jnp.where(retain, shaped, jnp.zeros_like(shaped)).reshape(dense_tile.shape)


def aligned(operand, amount, bit_count, mover):
    for level in range(bit_count):
        moved = mover(operand, level)
        chosen = (amount >> level) % 2 == 1
        operand = jnp.where(chosen, moved, operand)
    return operand


def contract(left_part, right_part):
    return lax.dot_general(
        left_part, right_part, (((0,), (0,)), ((), ())), preferred_element_type=jnp.float32
    )


def shards(weights, weight_flags, hamiltonian, ham_flags):
    row_count = lax.axis_size("row")
    bit_count = (row_count - 1).bit_length()
    row_index = lax.axis_index("row")
    col_index = lax.axis_index("col")
    pair_index = col_index // 2
    parity = col_index % 2
    w_masked = masked(weights, weight_flags)
    h_masked = masked(hamiltonian, ham_flags)
    ham_tile = aligned(
        h_masked,
        pair_index,
        bit_count,
        lambda operand, level: from_behind(operand, "row", -(1 << level)),
    )
    w_half = aligned(
        w_masked,
        row_index,
        bit_count,
        lambda operand, level: from_behind(operand, "col", -(2 << level)),
    )
    half_rows = ham_tile.shape[0] // 2
    upper_rows = ham_tile[:half_rows]
    lower_rows = ham_tile[half_rows:]
    retained = jnp.where(parity == 0, upper_rows, lower_rows)
    handed = jnp.where(parity == 0, lower_rows, upper_rows)
    received = from_partner(handed, "col", 0)
    joined = jnp.where(
        parity == 0,
        jnp.concatenate((retained, received), 1),
        jnp.concatenate((received, retained), 1),
    )
    summed = contract(w_half, joined)
    for step_index in range(1, STEPS):
        w_half = from_behind(w_half, "col", -2)
        joined = from_behind(joined, "row", -1)
        summed = summed + contract(w_half, joined)
    half_width = summed.shape[1] // 2
    own_part = jnp.where(parity == 0, summed[:, :half_width], summed[:, half_width:])
    their_part = jnp.where(parity == 0, summed[:, half_width:], summed[:, :half_width])
    summed = own_part + from_partner(their_part, "col", 0)
    return summed.astype(jnp.bfloat16)


SHARES = (1, 1, 1)
CHUNKS = len(SHARES)
MESH = pl.DeviceIdType.MESH


def put(source, target, sent, landed, device):
    return pltpu.make_async_remote_copy(
        src_ref=source,
        dst_ref=target,
        send_sem=sent,
        recv_sem=landed,
        device_id=device,
        device_id_type=MESH,
    )


def gather_kernel(
    panels, w_flags_hbm, h_flags_hbm, w_hbm, h_hbm, out_ref, w_flags, h_flags, w_ref, h_ref, w_buf, h_buf, total,
    loaded, w_landed, up_sent, down_sent, core_sent, h_landed, h_sent,
):
    row = lax.axis_index("row")
    col = lax.axis_index("col")
    pair = col // 2
    core = col % 2
    partner = (row, pair * 2 + 1 - core)
    above = (row, col + 2)
    below = (row, col - 2)
    beside = row + 1 - 2 * (row % 2)
    across = (row + panels // 2) % panels
    opposite = (beside + panels // 2) % panels
    has_above = pair < panels - 1
    has_below = pair > 0

    loads = [
        pltpu.make_async_copy(source, target, loaded.at[n])
        for n, (source, target) in enumerate(
            ((w_flags_hbm, w_flags), (w_hbm, w_ref), (h_flags_hbm, h_flags), (h_hbm, h_ref))
        )
    ]
    for load in loads:
        load.start()

    barrier = pltpu.get_barrier_semaphore()

    def greet(device):
        pl.semaphore_signal(barrier, inc=1, device_id=device, device_id_type=MESH)

    greet(partner)
    greet((beside, col))
    greet((across, col))

    @pl.when(has_above)
    def _():
        greet(above)

    @pl.when(has_below)
    def _():
        greet(below)

    loads[0].wait()
    loads[1].wait()
    half_rows, width = w_ref.shape
    edge = half_rows // w_flags.shape[0]
    bounds = [half_rows * sum(SHARES[:k]) // sum(SHARES) for k in range(CHUNKS + 1)]
    for r in range(w_flags.shape[0]):
        for c in range(w_flags.shape[1]):
            rows, lanes = slice(r * edge, (r + 1) * edge), slice(c * edge, (c + 1) * edge)
            block = w_ref[rows, lanes]
            kept = jnp.where(w_flags[r, c] > 0, block, jnp.zeros_like(block))
            w_buf[pair, core, rows, lanes] = kept
    pl.semaphore_wait(
        barrier, 3 + has_above.astype(jnp.int32) + has_below.astype(jnp.int32)
    )

    def piece(k):
        return slice(bounds[k], bounds[k + 1])

    def go_up(panel, k):
        slot = w_buf.at[panel, core, piece(k)]
        return put(slot, slot, up_sent.at[panel, k], w_landed.at[panel, core, k], above)

    def go_down(panel, k):
        slot = w_buf.at[panel, core, piece(k)]
        return put(slot, slot, down_sent.at[panel, k], w_landed.at[panel, core, k], below)

    def go_over(panel, k):
        slot = w_buf.at[panel, core, piece(k)]
        return put(slot, slot, core_sent.at[panel, k], w_landed.at[panel, core, k], partner)

    def arrival(panel, half, k):
        slot = w_buf.at[panel, half, piece(k)]
        return put(slot, slot, core_sent.at[panel, k], w_landed.at[panel, half, k], partner)

    def h_put(panel, half, number, device):
        slot = h_buf.at[panel, half]
        return put(slot, slot, h_sent.at[number], h_landed.at[panel, half], device)

    def each(body):
        for k in range(CHUNKS):
            body(k)

    def first_sends(k):
        @pl.when(has_above)
        def _():
            go_up(pair, k).start()

        @pl.when(has_below)
        def _():
            go_down(pair, k).start()

    each(first_sends)
    loads[2].wait()
    loads[3].wait()
    for r in range(h_flags.shape[1]):
        for c in range(h_flags.shape[0]):
            lanes = slice(c * edge, (c + 1) * edge)
            block = h_ref[r * edge:(r + 1) * edge, lanes]
            half, start = divmod(r * edge, half_rows)
            kept = jnp.where(h_flags[c, r] > 0, block, jnp.zeros_like(block))
            h_buf[row, half, start:start + edge, lanes] = kept

    h_copies = [
        h_put(row, 0, 0, (beside, col)),
        h_put(row, 1, 1, (across, col)),
        h_put(row, 1, 2, (beside, col)),
        h_put(row, 0, 3, (across, col)),
    ]
    for copy in h_copies:
        copy.start()
    each(lambda k: go_over(pair, k).start())

    def relay(distance, k):
        @pl.when(pair >= distance)
        def _():
            panel = pair - distance
            arrival(panel, core, k).wait_recv()

            @pl.when(has_above)
            def _():
                go_up(panel, k).start()

            go_over(panel, k).start()

        @pl.when(pair + distance < panels)
        def _():
            panel = pair + distance
            arrival(panel, core, k).wait_recv()

            @pl.when(has_below)
            def _():
                go_down(panel, k).start()

            go_over(panel, k).start()

    each(functools.partial(relay, 1))
    h_put(beside, 0, 0, (beside, col)).wait_recv()
    relay_across = h_put(beside, 0, 4, (across, col))
    relay_across.start()
    h_put(across, 1, 0, (beside, col)).wait_recv()
    relay_beside = h_put(across, 1, 5, (beside, col))
    relay_beside.start()
    for distance in range(2, panels - 1):
        each(functools.partial(relay, distance))
    h_put(beside, 1, 0, (beside, col)).wait_recv()
    h_put(across, 0, 0, (beside, col)).wait_recv()
    h_put(opposite, 0, 0, (beside, col)).wait_recv()
    h_put(opposite, 1, 0, (beside, col)).wait_recv()

    total[...] = jnp.zeros_like(total)
    span = 2 * half_rows

    def near_panel(step, carry):
        panel = (pair + step) % panels
        gap = panel - pair

        @pl.when((gap < panels - 1) & (gap > 1 - panels))
        def _():
            each(lambda k: arrival(panel, 1 - core, k).wait_recv())
            left = w_buf[panel].reshape(span, width)
            right = h_buf[panel].reshape(span, h_buf.shape[3])
            total[...] += contract(left, right)

        return carry

    lax.fori_loop(0, panels, near_panel, 0)

    is_end = (pair == 0) | (pair == panels - 1)

    @pl.when(is_end)
    def _():
        panel = panels - 1 - pair

        def product(half, k):
            return contract(w_buf[panel, half, piece(k)], h_buf[panel, half, piece(k)])

        for k in range(CHUNKS - 1):
            arrival(panel, core, k).wait_recv()
            go_over(panel, k).start()
            total[...] += product(core, k)
            arrival(panel, 1 - core, k).wait_recv()
            total[...] += product(1 - core, k)

        last = CHUNKS - 1
        arrival(panel, core, last).wait_recv()
        go_over(panel, last).start()
        total[...] += product(core, last)
        arrival(panel, 1 - core, last).wait_recv()
        out_ref[...] = (total[...] + product(1 - core, last)).astype(out_ref.dtype)

    @pl.when(jnp.logical_not(is_end))
    def _():
        out_ref[...] = total[...].astype(out_ref.dtype)

    for copy in h_copies + [relay_across, relay_beside]:
        copy.wait_send()

    def drain(panel, carry):
        def one(k):
            go_over(panel, k).wait_send()

            @pl.when(has_above & (panel <= pair))
            def _():
                go_up(panel, k).wait_send()

            @pl.when(has_below & (panel >= pair))
            def _():
                go_down(panel, k).wait_send()

        each(one)
        return carry

    lax.fori_loop(0, panels, drain, 0)


def gathered(weights, weight_flags, hamiltonian, ham_flags):
    panels = lax.axis_size("row")
    half_rows, width = weights.shape
    panel_rows, slice_cols = hamiltonian.shape
    dma = pltpu.SemaphoreType.DMA
    vmem = pl.BlockSpec(memory_space=pltpu.VMEM)
    hbm = pl.BlockSpec(memory_space=pl.ANY)
    return pl.pallas_call(
        functools.partial(gather_kernel, panels),
        out_shape=pltpu.VMEM((width, slice_cols), jnp.bfloat16),
        in_specs=[hbm] * 4,
        out_specs=vmem,
        scratch_shapes=[
            pltpu.SMEM(weight_flags.shape, weight_flags.dtype),
            pltpu.SMEM(ham_flags.shape[::-1], ham_flags.dtype),
            pltpu.VMEM(weights.shape, weights.dtype),
            pltpu.VMEM(hamiltonian.shape, hamiltonian.dtype),
            pltpu.VMEM((panels, 2, half_rows, width), jnp.bfloat16),
            pltpu.VMEM((panels, 2, panel_rows // 2, slice_cols), jnp.bfloat16),
            pltpu.VMEM((width, slice_cols), jnp.float32),
            dma((4,)),
            dma((panels, 2, CHUNKS)),
            dma((panels, CHUNKS)),
            dma((panels, CHUNKS)),
            dma((panels, CHUNKS)),
            dma((panels, 2)),
            dma((6,)),
        ],
        compiler_params=pltpu.CompilerParams(collective_id=0, has_side_effects=True),
    )(weight_flags, ham_flags.T, weights, hamiltonian)


def solution(mesh):
    placed = (P("col", "row"), P("col", "row"), P("row", "col"), P("row", "col"))
    every_panel = mesh.shape["row"] == STEPS and mesh.shape["col"] == 2 * STEPS
    return jax.shard_map(
        gathered if every_panel else shards,
        mesh=mesh, in_specs=placed, out_specs=P("row", "col"), check_vma=False,
    )
```

```python
import functools

import jax
import jax.numpy as jnp
from jax import lax
from jax.experimental import pallas as pl
from jax.experimental.pallas import tpu as pltpu
from jax.sharding import PartitionSpec as P

STEPS = 4


def from_behind(block, axis, distance):
    devices = range(lax.axis_size(axis))
    route = [((i - distance) % len(devices), i) for i in devices]
    return lax.ppermute(block, axis, route)


def from_partner(value, axis, bit):
    mask = 2**bit
    pairs = [(source, source ^ mask) for source in range(lax.axis_size(axis))]
    return lax.ppermute(value, axis, pairs)


def masked(dense_tile, flag_grid):
    row_blocks, col_blocks = flag_grid.shape
    block_edge = dense_tile.shape[0] // row_blocks
    shaped = dense_tile.reshape(row_blocks, block_edge, col_blocks, block_edge)
    retain = (flag_grid > 0)[:, None, :, None]
    return jnp.where(retain, shaped, jnp.zeros_like(shaped)).reshape(dense_tile.shape)


def aligned(operand, amount, bit_count, mover):
    for level in range(bit_count):
        moved = mover(operand, level)
        chosen = (amount >> level) % 2 == 1
        operand = jnp.where(chosen, moved, operand)
    return operand


def contract(left_part, right_part):
    return lax.dot_general(
        left_part, right_part, (((0,), (0,)), ((), ())), preferred_element_type=jnp.float32
    )


def shards(weights, weight_flags, hamiltonian, ham_flags):
    row_count = lax.axis_size("row")
    bit_count = (row_count - 1).bit_length()
    row_index = lax.axis_index("row")
    col_index = lax.axis_index("col")
    pair_index = col_index // 2
    parity = col_index % 2
    w_masked = masked(weights, weight_flags)
    h_masked = masked(hamiltonian, ham_flags)
    ham_tile = aligned(
        h_masked,
        pair_index,
        bit_count,
        lambda operand, level: from_behind(operand, "row", -(1 << level)),
    )
    w_half = aligned(
        w_masked,
        row_index,
        bit_count,
        lambda operand, level: from_behind(operand, "col", -(2 << level)),
    )
    half_rows = ham_tile.shape[0] // 2
    upper_rows = ham_tile[:half_rows]
    lower_rows = ham_tile[half_rows:]
    retained = jnp.where(parity == 0, upper_rows, lower_rows)
    handed = jnp.where(parity == 0, lower_rows, upper_rows)
    received = from_partner(handed, "col", 0)
    joined = jnp.where(
        parity == 0,
        jnp.concatenate((retained, received), 1),
        jnp.concatenate((received, retained), 1),
    )
    summed = contract(w_half, joined)
    for step_index in range(1, STEPS):
        w_half = from_behind(w_half, "col", -2)
        joined = from_behind(joined, "row", -1)
        summed = summed + contract(w_half, joined)
    half_width = summed.shape[1] // 2
    own_part = jnp.where(parity == 0, summed[:, :half_width], summed[:, half_width:])
    their_part = jnp.where(parity == 0, summed[:, half_width:], summed[:, :half_width])
    summed = own_part + from_partner(their_part, "col", 0)
    return summed.astype(jnp.bfloat16)


SHARES = (5, 3)
CHUNKS = len(SHARES)
MESH = pl.DeviceIdType.MESH


def put(source, target, sent, landed, device):
    return pltpu.make_async_remote_copy(
        src_ref=source,
        dst_ref=target,
        send_sem=sent,
        recv_sem=landed,
        device_id=device,
        device_id_type=MESH,
    )


def gather_kernel(
    panels, w_flags_hbm, h_flags_hbm, w_hbm, h_hbm, out_ref, w_flags, h_flags, w_ref, h_ref, w_buf, h_buf, total,
    loaded, w_landed, up_sent, down_sent, core_sent, h_landed, h_sent,
):
    row = lax.axis_index("row")
    col = lax.axis_index("col")
    pair = col // 2
    core = col % 2
    partner = (row, pair * 2 + 1 - core)
    above = (row, col + 2)
    below = (row, col - 2)
    beside = row + 1 - 2 * (row % 2)
    across = (row + panels // 2) % panels
    opposite = (beside + panels // 2) % panels
    has_above = pair < panels - 1
    has_below = pair > 0

    loads = [
        pltpu.make_async_copy(source, target, loaded.at[n])
        for n, (source, target) in enumerate(
            ((w_flags_hbm, w_flags), (w_hbm, w_ref), (h_flags_hbm, h_flags), (h_hbm, h_ref))
        )
    ]
    for load in loads:
        load.start()

    barrier = pltpu.get_barrier_semaphore()

    def greet(device):
        pl.semaphore_signal(barrier, inc=1, device_id=device, device_id_type=MESH)

    greet(partner)
    greet((beside, col))
    greet((across, col))

    @pl.when(has_above)
    def _():
        greet(above)

    @pl.when(has_below)
    def _():
        greet(below)

    loads[0].wait()
    loads[1].wait()
    half_rows, width = w_ref.shape
    edge = half_rows // w_flags.shape[0]
    bounds = [half_rows * sum(SHARES[:k]) // sum(SHARES) for k in range(CHUNKS + 1)]
    for r in range(w_flags.shape[0]):
        for c in range(w_flags.shape[1]):
            rows, lanes = slice(r * edge, (r + 1) * edge), slice(c * edge, (c + 1) * edge)
            block = w_ref[rows, lanes]
            kept = jnp.where(w_flags[r, c] > 0, block, jnp.zeros_like(block))
            w_buf[pair, core, rows, lanes] = kept
    pl.semaphore_wait(
        barrier, 3 + has_above.astype(jnp.int32) + has_below.astype(jnp.int32)
    )

    def piece(k):
        return slice(bounds[k], bounds[k + 1])

    def go_up(panel, k):
        slot = w_buf.at[panel, core, piece(k)]
        return put(slot, slot, up_sent.at[panel, k], w_landed.at[panel, core, k], above)

    def go_down(panel, k):
        slot = w_buf.at[panel, core, piece(k)]
        return put(slot, slot, down_sent.at[panel, k], w_landed.at[panel, core, k], below)

    def go_over(panel, k):
        slot = w_buf.at[panel, core, piece(k)]
        return put(slot, slot, core_sent.at[panel, k], w_landed.at[panel, core, k], partner)

    def arrival(panel, half, k):
        slot = w_buf.at[panel, half, piece(k)]
        return put(slot, slot, core_sent.at[panel, k], w_landed.at[panel, half, k], partner)

    def h_put(panel, half, number, device):
        slot = h_buf.at[panel, half]
        return put(slot, slot, h_sent.at[number], h_landed.at[panel, half], device)

    def each(body):
        for k in range(CHUNKS):
            body(k)

    def first_sends(k):
        @pl.when(has_above)
        def _():
            go_up(pair, k).start()

        @pl.when(has_below)
        def _():
            go_down(pair, k).start()

    each(first_sends)
    loads[2].wait()
    loads[3].wait()
    for r in range(h_flags.shape[1]):
        for c in range(h_flags.shape[0]):
            lanes = slice(c * edge, (c + 1) * edge)
            block = h_ref[r * edge:(r + 1) * edge, lanes]
            half, start = divmod(r * edge, half_rows)
            kept = jnp.where(h_flags[c, r] > 0, block, jnp.zeros_like(block))
            h_buf[row, half, start:start + edge, lanes] = kept

    h_copies = [
        h_put(row, 0, 0, (beside, col)),
        h_put(row, 1, 1, (across, col)),
        h_put(row, 1, 2, (beside, col)),
        h_put(row, 0, 3, (across, col)),
    ]
    for copy in h_copies:
        copy.start()
    each(lambda k: go_over(pair, k).start())

    def relay(distance, k):
        @pl.when(pair >= distance)
        def _():
            panel = pair - distance
            arrival(panel, core, k).wait_recv()

            @pl.when(has_above)
            def _():
                go_up(panel, k).start()

            go_over(panel, k).start()

        @pl.when(pair + distance < panels)
        def _():
            panel = pair + distance
            arrival(panel, core, k).wait_recv()

            @pl.when(has_below)
            def _():
                go_down(panel, k).start()

            go_over(panel, k).start()

    each(functools.partial(relay, 1))
    h_put(beside, 0, 0, (beside, col)).wait_recv()
    relay_across = h_put(beside, 0, 4, (across, col))
    relay_across.start()
    h_put(across, 1, 0, (beside, col)).wait_recv()
    relay_beside = h_put(across, 1, 5, (beside, col))
    relay_beside.start()
    for distance in range(2, panels - 1):
        each(functools.partial(relay, distance))
    h_put(beside, 1, 0, (beside, col)).wait_recv()
    h_put(across, 0, 0, (beside, col)).wait_recv()
    h_put(opposite, 0, 0, (beside, col)).wait_recv()
    h_put(opposite, 1, 0, (beside, col)).wait_recv()

    total[...] = jnp.zeros_like(total)
    span = 2 * half_rows

    def near_panel(step, carry):
        panel = (pair + step) % panels
        gap = panel - pair

        @pl.when((gap < panels - 1) & (gap > 1 - panels))
        def _():
            each(lambda k: arrival(panel, 1 - core, k).wait_recv())
            left = w_buf[panel].reshape(span, width)
            right = h_buf[panel].reshape(span, h_buf.shape[3])
            total[...] += contract(left, right)

        return carry

    lax.fori_loop(0, panels, near_panel, 0)

    is_end = (pair == 0) | (pair == panels - 1)

    @pl.when(is_end)
    def _():
        panel = panels - 1 - pair

        def product(half, k):
            return contract(w_buf[panel, half, piece(k)], h_buf[panel, half, piece(k)])

        for k in range(CHUNKS - 1):
            arrival(panel, core, k).wait_recv()
            go_over(panel, k).start()
            total[...] += product(core, k)
            arrival(panel, 1 - core, k).wait_recv()
            total[...] += product(1 - core, k)

        last = CHUNKS - 1
        arrival(panel, core, last).wait_recv()
        go_over(panel, last).start()
        total[...] += product(core, last)
        arrival(panel, 1 - core, last).wait_recv()
        out_ref[...] = (total[...] + product(1 - core, last)).astype(out_ref.dtype)

    @pl.when(jnp.logical_not(is_end))
    def _():
        out_ref[...] = total[...].astype(out_ref.dtype)

    for copy in h_copies + [relay_across, relay_beside]:
        copy.wait_send()

    def drain(panel, carry):
        def one(k):
            go_over(panel, k).wait_send()

            @pl.when(has_above & (panel <= pair))
            def _():
                go_up(panel, k).wait_send()

            @pl.when(has_below & (panel >= pair))
            def _():
                go_down(panel, k).wait_send()

        each(one)
        return carry

    lax.fori_loop(0, panels, drain, 0)


def gathered(weights, weight_flags, hamiltonian, ham_flags):
    panels = lax.axis_size("row")
    half_rows, width = weights.shape
    panel_rows, slice_cols = hamiltonian.shape
    dma = pltpu.SemaphoreType.DMA
    vmem = pl.BlockSpec(memory_space=pltpu.VMEM)
    hbm = pl.BlockSpec(memory_space=pl.ANY)
    return pl.pallas_call(
        functools.partial(gather_kernel, panels),
        out_shape=pltpu.VMEM((width, slice_cols), jnp.bfloat16),
        in_specs=[hbm] * 4,
        out_specs=vmem,
        scratch_shapes=[
            pltpu.SMEM(weight_flags.shape, weight_flags.dtype),
            pltpu.SMEM(ham_flags.shape[::-1], ham_flags.dtype),
            pltpu.VMEM(weights.shape, weights.dtype),
            pltpu.VMEM(hamiltonian.shape, hamiltonian.dtype),
            pltpu.VMEM((panels, 2, half_rows, width), jnp.bfloat16),
            pltpu.VMEM((panels, 2, panel_rows // 2, slice_cols), jnp.bfloat16),
            pltpu.VMEM((width, slice_cols), jnp.float32),
            dma((4,)),
            dma((panels, 2, CHUNKS)),
            dma((panels, CHUNKS)),
            dma((panels, CHUNKS)),
            dma((panels, CHUNKS)),
            dma((panels, 2)),
            dma((6,)),
        ],
        compiler_params=pltpu.CompilerParams(collective_id=0, has_side_effects=True),
    )(weight_flags, ham_flags.T, weights, hamiltonian)


def solution(mesh):
    placed = (P("col", "row"), P("col", "row"), P("row", "col"), P("row", "col"))
    every_panel = mesh.shape["row"] == STEPS and mesh.shape["col"] == 2 * STEPS
    return jax.shard_map(
        gathered if every_panel else shards,
        mesh=mesh, in_specs=placed, out_specs=P("row", "col"), check_vma=False,
    )
```
